256 devices in a mesh: gx: 16 (over z, x_hi), gy: 16 (over y, x_lo, core).
Axes of the slice: x: 4 (x_hi: 2, x_lo: 2; x = x_hi * 2 + x_lo), y: 4, z: 8, core: 2. Of those that a mesh axis runs over, the one named last changes fastest.
Arguments:
- f_in: float32 [19, 16, 256, 2048], P(None, None, 'gx', 'gy')
- rotor_place: int32 [40, 3], replicated, may hold values from 0 to 15, as said below
- marker_cell: int32 [40, 8192], replicated, may hold values from 16384 to 2078527, as said below
- pitch_phase: int32 [40, 2], replicated, may hold values from 0 to 63
- blade_area: float32 [16, 16, 2, 8192], P('gx', 'gy'), may hold values from 0.3 to 1.2
- blade_twist: float32 [16, 16, 2, 8192], P('gx', 'gy'), may hold values from -0.6 to 0.6
- blade_speed: float32 [16, 16, 2, 8192], P('gx', 'gy'), may hold values from 1.5 to 3
- blade_angle: float32 [16, 16, 2, 8192], P('gx', 'gy'), may hold values from -3.14 to 3.14, as said below
- filt_in: float32 [16, 16, 2, 3, 8192], P('gx', 'gy'), may hold values from -1.5 to 1.5
Outputs:
- f_out: float32 [19, 16, 256, 2048], P(None, None, 'gx', 'gy')
- loads_out: float32 [16, 16, 2, 3, 8192], P('gx', 'gy')
- filt_out: float32 [16, 16, 2, 3, 8192], P('gx', 'gy')
The draws below stay inside these ranges and needn't reach their ends.
Inputs may be any that keep to these rules, and one draw needn't show every extreme that they name: `rotor_place`: column 0 is a streamwise tile holding at most 3 rotors, some exactly 3; column 1 a plane 0 to 15; column 2 the owner's spanwise tile. Every streamwise tile holds 2 or more rotors; one owner holds at most 2 rotors, exactly 2 in every streamwise tile. `marker_cell`: all stencil cells of one rotor lie within two neighbouring spanwise tiles and within levels 0 to 15; a rotor's stencils may cover one or two tiles. `blade_angle`: azimuths in radians.
All inputs are finite; a program needn't handle non-finite values.
Results may differ from the reference program's by a relative error of at most 0.0003.
Values sent between devices are 32-bit elements; how exact they have to be, the bound alone decides.
A program may use at most 128 MiB of HBM per device.

```python
import math
import jax
import jax.numpy as jnp
import numpy as np
from jax import lax

CX = 16
CY = 128
Z = 16
M = 8192
ROTORS = 40
STEPS = 2
OSLOT = 2
PHASES = 64
TX = 16
TY = 16
NX = 256
NY = 2048
HALF = 48


LATTICE_DIRS = np.array([[0, 0, 0], [1, 0, 0], [-1, 0, 0], [0, 1, 0], [0, -1, 0], [0, 0, 1], [0, 0, -1], [1, 1, 0], [-1, -1, 0], [1, -1, 0], [-1, 1, 0], [1, 0, 1], [-1, 0, -1], [1, 0, -1], [-1, 0, 1], [0, 1, 1], [0, -1, -1], [0, 1, -1], [0, -1, 1]])


LATTICE_WEIGHTS = np.array([1.0 / 3.0] + [1.0 / 18.0] * 6 + [1.0 / 36.0] * 12)


def geometry(key):
    base_key = jax.random.fold_in(key, 7)
    subkeys = jax.random.split(base_key, 8)
    shuffle = jax.random.permutation(subkeys[0], ROTORS)
    street = (jnp.argsort(shuffle) % TX).astype(jnp.int32)
    rotor_ids = jnp.arange(ROTORS, dtype=jnp.int32)
    earlier = rotor_ids[None, :] < rotor_ids[:, None]
    same_row = street[:, None] == street[None, :]
    row_rank = jnp.sum((earlier & same_row).astype(jnp.int32), axis=1)
    first_owner = jax.random.randint(subkeys[1], (TX,), 0, TY)
    owner_y = ((first_owner[street] + row_rank // 2) % TY).astype(jnp.int32)
    plane_x = jax.random.randint(subkeys[2], (ROTORS,), 0, CX)
    plane_x = plane_x.at[0].set(CX - 1)
    first_tile = jax.random.randint(subkeys[3], (ROTORS,), 0, TY - 1)
    first_tile = first_tile.at[0].set(TY - 2).at[1].set(0)
    offset = jax.random.randint(subkeys[4], (ROTORS,), -(CY // 2), CY // 2 + 1)
    offset = offset.at[0].set(CY // 2).at[1].set(-(CY // 2))
    centre = (first_tile + 1) * CY + offset
    cell_y = centre[:, None] - HALF + jax.random.randint(subkeys[5], (ROTORS, M), 0, 2 * HALF - 2)
    cell_y = cell_y.at[:, 0].set(centre - HALF).at[:, 1].set(centre + HALF - 3)
    cell_z = jax.random.randint(subkeys[6], (ROTORS, M), 0, Z - 3)
    cell_z = cell_z.at[0, 1].set(Z - 4).at[1, 0].set(0)
    fractions = jax.random.randint(subkeys[7], (ROTORS, M), 0, 64)
    fractions = fractions.at[0, 1].set(63).at[1, 0].set(0)
    cell_codes = ((cell_y * Z + cell_z) * 64 + fractions).astype(jnp.int32)
    place = jnp.stack([street, plane_x.astype(jnp.int32), owner_y], axis=1)
    return (place, cell_codes)


def draw_rotor_place(key, part):
    place, cell_codes = geometry(key)
    return place


def draw_marker_cell(key, part):
    place, cell_codes = geometry(key)
    return cell_codes


def draw_blade_angle(key, part):
    subkeys = jax.random.split(jax.random.fold_in(key, 11), 3)
    side = (2 * jax.random.randint(subkeys[0], (TX, TY, OSLOT, 1), 0, 2) - 1).astype(jnp.float32)
    centre_spread = 0.4
    marker_spread = 0.5
    centre_shift = jax.random.uniform(subkeys[1], (TX, TY, OSLOT, 1), jnp.float32, -centre_spread, centre_spread)
    wobble = jax.random.uniform(subkeys[2], (TX, TY, OSLOT, M), jnp.float32, -marker_spread, marker_spread)
    return side * (0.5 * math.pi + centre_shift) + wobble


def draw_f_in(key, part):
    subkeys = jax.random.split(key, 7)
    shape = (Z, NX, NY)
    x_ids = jnp.arange(NX, dtype=jnp.int32)
    phase = jax.random.randint(subkeys[5], (), 0, 2)
    pattern = (1 - 2 * ((x_ids + phase) % 2)).astype(jnp.float32)
    density = jax.random.uniform(subkeys[0], shape, jnp.float32, 0.9, 1.1)
    plane_noise = jax.random.uniform(subkeys[6], (NX,), jnp.float32, -0.03, 0.03)
    axial_speed = 0.08 + (0.07 * pattern + plane_noise)[None, :, None] + jax.random.uniform(subkeys[1], shape, jnp.float32, -0.03, 0.03)
    span_speed = jax.random.uniform(subkeys[2], shape, jnp.float32, -0.05, 0.05)
    lift_speed = jax.random.uniform(subkeys[3], shape, jnp.float32, -0.05, 0.05)
    jitter = jax.random.uniform(subkeys[4], (19,) + shape, jnp.float32, -0.05, 0.05)
    lattice = jnp.asarray(LATTICE_DIRS, jnp.float32)
    weights = jnp.asarray(LATTICE_WEIGHTS, jnp.float32)[:, None, None, None]
    project = lattice[:, 0][:, None, None, None] * axial_speed[None] + lattice[:, 1][:, None, None, None] * span_speed[None] + lattice[:, 2][:, None, None, None] * lift_speed[None]
    speed_sq = axial_speed * axial_speed + span_speed * span_speed + lift_speed * lift_speed
    equilibrium = weights * density[None] * (1.0 + 3.0 * project + 4.5 * project * project - 1.5 * speed_sq[None])
    return equilibrium * (1.0 + jitter)


def set_ends(result, own_key, low, high):
    shape = result.shape
    spot = [jax.random.randint(jax.random.fold_in(own_key, axis), (), 0, shape[axis]) for axis in range(len(shape))]
    result = result.at[tuple(spot)].set(low)
    longest = shape.index(max(shape))
    spot[longest] = (spot[longest] + 1) % shape[longest]
    return result.at[tuple(spot)].set(high)


def block_scale(rng, extent, shards, smallest, high):
    gain = 1.0
    for axis_at, shards_of in shards:
        draws = jax.random.uniform(jax.random.fold_in(jax.random.fold_in(rng, 6), axis_at), (shards_of,), jnp.float32, smallest / len(shards), high / len(shards))
        gain = gain * jnp.repeat(jnp.exp(draws), extent[axis_at] // shards_of).reshape((-1,) + (1,) * (len(extent) - 1 - axis_at))
    return gain


def centred(stream_key, shape, scale, reach, pieces=(), kind=jnp.bfloat16):
    gain = block_scale(stream_key, shape, pieces, -0.22, 0.18) if pieces else 1.0
    drawn = jax.random.normal(stream_key, shape, jnp.float32) * scale * gain
    return jnp.minimum(jnp.maximum(drawn, -reach), reach).astype(kind)


def setup_inputs(seed: int = 0) -> dict:
    key_of = jax.random.split(jax.random.key(seed), 10)
    return {
        "f_in": draw_f_in(jax.random.fold_in(key_of[9], 71), 0),
        "rotor_place": draw_rotor_place(jax.random.fold_in(key_of[9], 71), 0),
        "marker_cell": draw_marker_cell(jax.random.fold_in(key_of[9], 71), 0),
        "pitch_phase": set_ends(jax.random.randint(key_of[3], (ROTORS, STEPS), 0, PHASES), jax.random.fold_in(key_of[3], 1), 0, PHASES - 1).astype(jnp.int32),
        "blade_area": jnp.clip(jnp.exp(math.log(1.2) - 1.3862944 * jax.random.uniform(key_of[4], (TX, TY, OSLOT, M), jnp.float32) ** block_scale(key_of[4], (TX, TY, OSLOT, M), ((0, 16), (1, 16)), -0.2, 0.2)), 0.3, 1.2),
        "blade_twist": jnp.clip(jax.random.uniform(key_of[5], (TX, TY, OSLOT, M), jnp.float32, -0.6, 0.6) * block_scale(key_of[5], (TX, TY, OSLOT, M), ((0, 16), (1, 16)), -0.4, 0.0), -0.6, 0.6),
        "blade_speed": jnp.clip(jnp.exp(math.log(3.0) - 0.6931472 * jax.random.uniform(key_of[6], (TX, TY, OSLOT, M), jnp.float32) ** block_scale(key_of[6], (TX, TY, OSLOT, M), ((0, 16), (1, 16)), -0.2, 0.2)), 1.5, 3.0),
        "blade_angle": draw_blade_angle(jax.random.fold_in(key_of[9], 71), 0),
        "filt_in": centred(key_of[8], (TX, TY, OSLOT, 3, M), 0.1, 1.5, ((0, 16), (1, 16)), jnp.float32),
    }


LATTICE_DIRS = np.array([[0, 0, 0], [1, 0, 0], [-1, 0, 0], [0, 1, 0], [0, -1, 0], [0, 0, 1], [0, 0, -1], [1, 1, 0], [-1, -1, 0], [1, -1, 0], [-1, 1, 0], [1, 0, 1], [-1, 0, -1], [1, 0, -1], [-1, 0, 1], [0, 1, 1], [0, -1, -1], [0, 1, -1], [0, -1, 1]])
OPPOSITE = [0, 2, 1, 4, 3, 6, 5, 8, 7, 10, 9, 12, 11, 14, 13, 16, 15, 18, 17]
LATTICE_WEIGHTS = np.array([1.0 / 3.0] + [1.0 / 18.0] * 6 + [1.0 / 36.0] * 12)
OMEGA = 1.0 / 0.6
SPREAD = 0.01
MIX = 0.5
PITCH_AMP = 0.2

def peskin(offsets):
    distance = jnp.abs(offsets)
    near_arg = jnp.maximum(1.0 + 4.0 * distance - 4.0 * distance * distance, 1.0)
    far_arg = jnp.maximum(-7.0 + 12.0 * distance - 4.0 * distance * distance, 1.0)
    near_part = (3.0 - 2.0 * distance + jnp.sqrt(near_arg)) / 8.0
    far_part = (5.0 - 2.0 * distance - jnp.sqrt(far_arg)) / 8.0
    return jnp.where(distance <= 1.0, near_part, far_part)

def dense_rows(anchor, weights, width, start):
    column = jnp.arange(width, dtype=jnp.int32)[None, :] + start
    gap = column - anchor[:, None]
    summed = jnp.zeros(gap.shape, jnp.float32)
    for corner in range(4):
        summed = summed + jnp.where(gap == corner, weights[corner][:, None], 0.0)
    return summed

def stencil_tables(cell_codes, levels, width, start):
    fraction_z = (cell_codes % 8).astype(jnp.float32) / 8.0
    fraction_y = (cell_codes // 8 % 8).astype(jnp.float32) / 8.0
    cell_z = (cell_codes // 64 % levels).astype(jnp.int32)
    cell_y = (cell_codes // (64 * levels)).astype(jnp.int32)
    weights_y = [peskin(corner - 1.0 - fraction_y) for corner in range(4)]
    weights_z = [peskin(corner - 1.0 - fraction_z) for corner in range(4)]
    across = dense_rows(cell_y, weights_y, width, start)
    upward = dense_rows(cell_z, weights_z, levels, jnp.int32(0))
    return (across, upward)

def sample_section(section, across, upward):
    levels = section.shape[1]
    width = section.shape[2]
    flattened = jnp.transpose(section, (2, 0, 1)).reshape(width, 3 * levels)
    partial_value = jnp.dot(across, flattened, precision=lax.Precision.HIGHEST, preferred_element_type=jnp.float32)
    partial_value = partial_value.reshape(across.shape[0], 3, levels)
    return jnp.transpose(lax.optimization_barrier(jnp.sum(partial_value * upward[:, None, :], axis=2)))

def spread_section(marker_loads, across, upward):
    markers = upward.shape[0]
    levels = upward.shape[1]
    weighted = (upward[:, None, :] * jnp.transpose(marker_loads)[:, :, None]).reshape(markers, 3 * levels)
    section = lax.dot_general(weighted, across, (((0,), (0,)), ((), ())), precision=lax.Precision.HIGHEST, preferred_element_type=jnp.float32)
    return -SPREAD * section.reshape(3, levels, across.shape[1])

def pitch_angles(phases):
    return PITCH_AMP * jnp.sin(2.0 * math.pi * phases.astype(jnp.float32) / PHASES)

def blade_loads(filtered, area, twist, speed, angle, pitch):
    axial_speed = filtered[..., 0, :]
    sin_t = jnp.sin(angle)
    cos_t = jnp.cos(angle)
    tangent = speed + sin_t * filtered[..., 1, :] - cos_t * filtered[..., 2, :]
    square = axial_speed * axial_speed + tangent * tangent
    magnitude = jnp.sqrt(square)
    sin_p = axial_speed / magnitude
    cos_p = tangent / magnitude
    blade_pitch = twist + pitch
    sin_a = sin_p * jnp.cos(blade_pitch) - cos_p * jnp.sin(blade_pitch)
    cos_a = cos_p * jnp.cos(blade_pitch) + sin_p * jnp.sin(blade_pitch)
    lift_coef = 2.0 * math.pi * sin_a * cos_a
    drag_coef = 0.02 + sin_a * sin_a
    dynamic = 0.5 * area * square
    normal = dynamic * (lift_coef * cos_p + drag_coef * sin_p)
    tangential = dynamic * (lift_coef * sin_p - drag_coef * cos_p)
    return jnp.stack([normal, -tangential * sin_t, tangential * cos_t], axis=-2)

def velocity(populations):
    lattice = jnp.asarray(LATTICE_DIRS, jnp.float32)
    density = lax.optimization_barrier(jnp.sum(populations, axis=0))
    parts = [lax.optimization_barrier(jnp.sum(populations * lattice[:, axis][:, None, None, None], axis=0)) / density for axis in range(3)]
    return jnp.stack(parts)

def collide(populations, force_field):
    lattice = jnp.asarray(LATTICE_DIRS, jnp.float32)
    weights = jnp.asarray(LATTICE_WEIGHTS, jnp.float32)[:, None, None, None]
    density = lax.optimization_barrier(jnp.sum(populations, axis=0))
    columns = [lattice[:, axis][:, None, None, None] for axis in range(3)]
    parts = [(lax.optimization_barrier(jnp.sum(populations * columns[axis], axis=0)) + 0.5 * force_field[axis]) / density for axis in range(3)]
    project = columns[0] * parts[0][None] + columns[1] * parts[1][None] + columns[2] * parts[2][None]
    force_proj = columns[0] * force_field[0][None] + columns[1] * force_field[1][None] + columns[2] * force_field[2][None]
    speed_sq = parts[0] * parts[0] + parts[1] * parts[1] + parts[2] * parts[2]
    work_rate = parts[0] * force_field[0] + parts[1] * force_field[1] + parts[2] * force_field[2]
    equilibrium = weights * density[None] * (1.0 + 3.0 * project + 4.5 * project * project - 1.5 * speed_sq[None])
    source = (1.0 - 0.5 * OMEGA) * weights * (3.0 * (force_proj - work_rate[None]) + 9.0 * project * force_proj)
    return populations - OMEGA * (populations - equilibrium) + source

def stream(padded, collided):
    x_cells = collided.shape[2]
    y_cells = collided.shape[3]
    outgoing = []
    for direction in range(19):
        shift_x = int(LATTICE_DIRS[direction, 0])
        shift_y = int(LATTICE_DIRS[direction, 1])
        shift_z = int(LATTICE_DIRS[direction, 2])
        pulled = padded[direction, :, 1 - shift_x:1 - shift_x + x_cells, 1 - shift_y:1 - shift_y + y_cells]
        mirror = collided[OPPOSITE[direction]]
        if shift_z == 1:
            pulled = jnp.concatenate([mirror[:1], pulled[:-1]], axis=0)
        elif shift_z == -1:
            pulled = jnp.concatenate([pulled[1:], mirror[-1:]], axis=0)
        outgoing.append(pulled)
    return jnp.stack(outgoing)

def reference(f_in, rotor_place, marker_cell, pitch_phase, blade_area, blade_twist, blade_speed, blade_angle, filt_in):
    street = rotor_place[:, 0]
    plane_x = rotor_place[:, 1]
    owner_y = rotor_place[:, 2]
    rotor_ids = jnp.arange(ROTORS, dtype=jnp.int32)
    earlier = rotor_ids[None, :] < rotor_ids[:, None]
    same_owner = (street[:, None] == street[None, :]) & (owner_y[:, None] == owner_y[None, :])
    owner_rank = lax.optimization_barrier(jnp.sum((earlier & same_owner).astype(jnp.int32), axis=1))
    filtered = filt_in[street, owner_y, owner_rank]
    area = blade_area[street, owner_y, owner_rank]
    twist = blade_twist[street, owner_y, owner_rank]
    speed = blade_speed[street, owner_y, owner_rank]
    angle = blade_angle[street, owner_y, owner_rank]
    pitch = pitch_angles(pitch_phase)
    lowest = lax.optimization_barrier(jnp.min(marker_cell // (64 * Z), axis=1))
    window = jnp.minimum(lowest // CY * CY, NY - 2 * CY).astype(jnp.int32)
    plane_global = (street * CX + plane_x).astype(jnp.int32)
    zero = jnp.int32(0)
    populations = f_in
    loads = jnp.zeros((ROTORS, 3, M), jnp.float32)
    for step_index in range(STEPS):
        field_speed = velocity(populations)

        def sample_one(inputs):
            cell_codes, place, start = inputs
            section = lax.dynamic_slice(field_speed, (zero, zero, place, start), (3, Z, 1, 2 * CY))[:, :, 0, :]
            across, upward = stencil_tables(cell_codes, Z, 2 * CY, start)
            return sample_section(section, across, upward)
        sampled = lax.map(sample_one, (marker_cell, plane_global, window))
        filtered = filtered + MIX * (sampled - filtered)
        loads = blade_loads(filtered, area, twist, speed, angle, pitch[:, step_index][:, None])

        def spread_one(force_field, inputs):
            cell_codes, place, start, rotor_loads = inputs
            across, upward = stencil_tables(cell_codes, Z, 2 * CY, start)
            section = spread_section(rotor_loads, across, upward)
            current = lax.dynamic_slice(force_field, (zero, zero, place, start), (3, Z, 1, 2 * CY))
            return (lax.dynamic_update_slice(force_field, current + section[:, :, None, :], (zero, zero, place, start)), None)
        force_field, unused = lax.scan(spread_one, jnp.zeros((3, Z, NX, NY), jnp.float32), (marker_cell, plane_global, window, loads))
        collided = collide(populations, force_field)
        padded = jnp.pad(collided, ((0, 0), (0, 0), (1, 1), (1, 1)), mode='wrap')
        populations = stream(padded, collided)
    loads_out = jnp.zeros((TX, TY, OSLOT, 3, M), jnp.float32).at[street, owner_y, owner_rank].set(loads)
    filt_out = jnp.zeros((TX, TY, OSLOT, 3, M), jnp.float32).at[street, owner_y, owner_rank].set(filtered)
    return (populations, loads_out, filt_out)
```

```python
import functools
import math

import jax
import jax.numpy as jnp
import numpy as np
from jax import lax
from jax.experimental import pallas as pl
from jax.experimental.pallas import tpu as pltpu
from jax.sharding import PartitionSpec as P

DIRS = [
    (0, 0, 0),
    (1, 0, 0), (-1, 0, 0), (0, 1, 0), (0, -1, 0), (0, 0, 1), (0, 0, -1),
    (1, 1, 0), (-1, -1, 0), (1, -1, 0), (-1, 1, 0),
    (1, 0, 1), (-1, 0, -1), (1, 0, -1), (-1, 0, 1),
    (0, 1, 1), (0, -1, -1), (0, 1, -1), (0, -1, 1),
]
OPPOSITE = [0, 2, 1, 4, 3, 6, 5, 8, 7, 10, 9, 12, 11, 14, 13, 16, 15, 18, 17]
WEIGHTS = [1.0 / 3.0] + [1.0 / 18.0] * 6 + [1.0 / 36.0] * 12
PAIRS = [(1, 2), (3, 4), (5, 6), (7, 8), (9, 10), (11, 12), (13, 14), (15, 16), (17, 18)]
OMEGA = 1.0 / 0.6
SPREAD = 0.01
MIX = 0.5
PITCH_AMP = 0.2
PHASES = 64

NQ = 19
LEVELS = 16
CX = 16
CY = 128
SLOTS = 3
ROWS = SLOTS * 2 * 3 * LEVELS
REDUCERS = 12
SHARD = ROWS // REDUCERS
TILES = 16
F32 = jnp.float32
MESH = pl.DeviceIdType.MESH

X_PLUS = [q for q in range(NQ) if DIRS[q][0] == 1]
X_MINUS = [q for q in range(NQ) if DIRS[q][0] == -1]
Y_PLUS = [q for q in range(NQ) if DIRS[q][1] == 1]
Y_MINUS = [q for q in range(NQ) if DIRS[q][1] == -1]


def peskin(offsets):
    distance = jnp.abs(offsets)
    near_arg = jnp.maximum(1.0 + 4.0 * distance - 4.0 * distance * distance, 1.0)
    far_arg = jnp.maximum(-7.0 + 12.0 * distance - 4.0 * distance * distance, 1.0)
    near_part = (3.0 - 2.0 * distance + jnp.sqrt(near_arg)) / 8.0
    far_part = (5.0 - 2.0 * distance - jnp.sqrt(far_arg)) / 8.0
    return jnp.where(distance <= 1.0, near_part, far_part)


def signed_sum(terms):
    total = None
    for sign, value in terms:
        if total is None:
            total = value if sign > 0 else -value
        else:
            total = total + value if sign > 0 else total - value
    return total


def moments(pops):
    density = pops[0]
    for q in range(1, NQ):
        density = density + pops[q]
    momentum = [
        signed_sum([(DIRS[q][axis], pops[q]) for q in range(NQ) if DIRS[q][axis] != 0])
        for axis in range(3)
    ]
    return density, momentum


def along(direction, vector):
    return signed_sum([(direction[axis], vector[axis]) for axis in range(3) if direction[axis]])


def collide(pops, force):
    density, momentum = moments(pops)
    inverse = 1.0 / density
    if force is not None:
        momentum = [momentum[axis] + 0.5 * force[axis] for axis in range(3)]
    vel = [momentum[axis] * inverse for axis in range(3)]
    speed_sq = vel[0] * vel[0] + vel[1] * vel[1] + vel[2] * vel[2]
    keep = 1.0 - OMEGA
    scaled = OMEGA * density
    base = scaled * (1.0 - 1.5 * speed_sq)
    if force is not None:
        half = 1.0 - 0.5 * OMEGA
        work = vel[0] * force[0] + vel[1] * force[1] + vel[2] * force[2]
        base = base - (3.0 * half) * work
    out = [None] * NQ
    out[0] = keep * pops[0] + WEIGHTS[0] * base
    for first, second in PAIRS:
        project = along(DIRS[first], vel)
        even = base + scaled * (4.5 * project * project)
        odd = scaled * (3.0 * project)
        if force is not None:
            pull = along(DIRS[first], force)
            even = even + (9.0 * half) * (project * pull)
            odd = odd + (3.0 * half) * pull
        weight = WEIGHTS[first]
        out[first] = keep * pops[first] + weight * (even + odd)
        out[second] = keep * pops[second] + weight * (even - odd)
    return out


def split(value):
    high = value.astype(jnp.bfloat16)
    low = (value - high.astype(F32)).astype(jnp.bfloat16)
    return high, low


def mega(
    f_ref, rp_ref, mc_ref, pp_ref, area_ref, twist_ref, speed_ref, angle_ref, filt_ref,
    fo_ref, lo_ref, io_ref,
    post, fnext, plane_f, plane_p, win_tx, rs_rx, win_rx, bl_tx, bl_rx, ou_tx, ou_rx,
    w_hi, w_lo, up_ref, val_ref,
    xs_tx, xs_rx, ys_tx, ys_rx, cr_rx,
    rs_s, rs_r, ag_s, ag_r, bl_s, bl_r, ou_s, ou_r, ha_s, ha_r,
):
    me_x = lax.axis_index("gx")
    me = lax.axis_index("gy")
    count_x = lax.axis_size("gx")
    steps = pp_ref.shape[1]
    rotors = rp_ref.shape[0]
    chunk = bl_tx.shape[3]
    x_up = lax.rem(me_x + 1, count_x)
    x_dn = lax.rem(me_x + count_x - 1, count_x)
    y_up = lax.rem(me + 1, TILES)
    y_dn = lax.rem(me + TILES - 1, TILES)

    barrier = pltpu.get_barrier_semaphore()

    def greet(k, carry):
        pl.semaphore_signal(
            barrier, inc=1, device_id={"gy": lax.rem(me + k, TILES)}, device_id_type=MESH
        )
        return carry

    lax.fori_loop(1, TILES, greet, 0)
    for other_x in (x_up, x_dn):
        pl.semaphore_signal(barrier, inc=1, device_id={"gx": other_x}, device_id_type=MESH)
        for other_y in (y_up, y_dn):
            pl.semaphore_signal(
                barrier, inc=1, device_id={"gx": other_x, "gy": other_y}, device_id_type=MESH
            )

    def exchange_start(src, dst, send, recv):
        def body(k, carry):
            to = lax.rem(me + k, TILES)
            pltpu.make_async_remote_copy(
                src_ref=src(to), dst_ref=dst, send_sem=send.at[k], recv_sem=recv.at[k],
                device_id={"gy": to}, device_id_type=MESH,
            ).start()
            return carry

        lax.fori_loop(1, TILES, body, 0)

    def exchange_wait(ref, sems, which):
        def body(k, carry):
            handle = pltpu.make_async_remote_copy(
                src_ref=ref, dst_ref=ref, send_sem=sems.at[k], recv_sem=sems.at[k],
                device_id={"gy": lax.rem(me + k, TILES)}, device_id_type=MESH,
            )
            if which == "recv":
                handle.wait_recv()
            else:
                handle.wait_send()
            return carry

        lax.fori_loop(1, TILES, body, 0)

    def reducer_of(tile):
        return lax.rem(tile, 4) < 3, (tile // 4) * 3 + lax.rem(tile, 4)

    is_reducer, my_shard = reducer_of(me)

    def scatter_start(turn):
        def body(k, carry):
            to = lax.rem(me + k, TILES)
            active, shard = reducer_of(to)

            @pl.when(active)
            def _():
                pltpu.make_async_remote_copy(
                    src_ref=win_tx.at[turn, shard], dst_ref=rs_rx.at[turn, me],
                    send_sem=rs_s.at[turn, k], recv_sem=rs_r.at[turn, k],
                    device_id={"gy": to}, device_id_type=MESH,
                ).start()

            return carry

        lax.fori_loop(1, TILES, body, 0)

    def scatter_finish(turn):
        @pl.when(is_reducer)
        def _():
            exchange_wait(rs_rx.at[turn, 0], rs_r.at[turn], "recv")
            rs_rx[turn, me] = win_tx[turn, my_shard]
            total = rs_rx[turn, 0]
            for source in range(1, TILES):
                total = total + rs_rx[turn, source]
            win_rx[turn, my_shard] = total
            exchange_start(
                lambda to: win_rx.at[turn, my_shard], win_rx.at[turn, my_shard],
                ag_s.at[turn], ag_r.at[turn],
            )

    def gather_wait(turn):
        def body(k, carry):
            source = lax.rem(me - k + TILES, TILES)
            active, shard = reducer_of(source)

            @pl.when(active)
            def _():
                pltpu.make_async_remote_copy(
                    src_ref=win_rx.at[turn, 0], dst_ref=win_rx.at[turn, 0],
                    send_sem=ag_s.at[turn, k], recv_sem=ag_r.at[turn, k],
                    device_id={"gy": source}, device_id_type=MESH,
                ).wait_recv()

            return carry

        lax.fori_loop(1, TILES, body, 0)

    def sends_done(turn):
        def body(k, carry):
            active, shard = reducer_of(lax.rem(me + k, TILES))

            @pl.when(active)
            def _():
                pltpu.make_async_remote_copy(
                    src_ref=win_tx.at[turn, 0], dst_ref=win_tx.at[turn, 0],
                    send_sem=rs_s.at[turn, k], recv_sem=rs_r.at[turn, k],
                    device_id={"gy": lax.rem(me + k, TILES)}, device_id_type=MESH,
                ).wait_send()

            return carry

        lax.fori_loop(1, TILES, body, 0)

        @pl.when(is_reducer)
        def _():
            exchange_wait(win_rx.at[turn, 0], ag_s.at[turn], "send")

    def find(r, carry):
        count, ids, planes, owners = carry
        here = (rp_ref[r, 0] == me_x).astype(jnp.int32)
        new_ids, new_planes, new_owners = [], [], []
        for s in range(SLOTS):
            take = here * (count == s).astype(jnp.int32)
            new_ids.append(ids[s] + take * r)
            new_planes.append(planes[s] + take * rp_ref[r, 1])
            new_owners.append(owners[s] + take * rp_ref[r, 2])
        return count + here, tuple(new_ids), tuple(new_planes), tuple(new_owners)

    zero = jnp.int32(0)
    count, ids, planes, owners = lax.fori_loop(
        0, rotors, find, (zero, (zero,) * SLOTS, (zero,) * SLOTS, (zero,) * SLOTS)
    )
    valid = [(count > s).astype(jnp.int32) for s in range(SLOTS)]
    ranks = [
        jnp.minimum(sum([(owners[s] == owners[e]).astype(jnp.int32) for e in range(s)], zero), 1)
        for s in range(SLOTS)
    ]

    firsts = []
    for s in range(SLOTS):
        codes = mc_ref[pl.ds(ids[s], 1), :]
        lowest = jnp.min(codes, axis=1, keepdims=True)
        firsts.append(jnp.minimum(lowest // (64 * LEVELS * CY), TILES - 2))

    level_shape = (LEVELS, CY)

    def sections(source, turn):
        for s in range(SLOTS):
            pops = [source[q, :, planes[s], :] for q in range(NQ)]
            for q in range(NQ):
                plane_f[s, q] = pops[q]
            density, momentum = moments(pops)
            inverse = 1.0 / density
            first = jnp.broadcast_to(firsts[s], level_shape)
            for half in range(2):
                inside = first == me - half
                for axis in range(3):
                    row = s * 96 + half * 48 + axis * LEVELS
                    value = jnp.where(inside, momentum[axis] * inverse, 0.0)
                    for part in range(2):
                        at = row + 8 * part
                        win_tx[turn, at // SHARD, at % SHARD : at % SHARD + 8, :] = value[
                            8 * part : 8 * part + 8
                        ]

    def window(turn, s, half):
        parts = []
        for block in range(6):
            at = s * 96 + half * 48 + 8 * block
            parts.append(win_rx[turn, at // SHARD, at % SHARD : at % SHARD + 8, :])
        return jnp.concatenate(parts, axis=0)

    def collide_levels(source, low, high):
        def body(z, carry):
            out = collide([source[q, z] for q in range(NQ)], None)
            for q in range(NQ):
                post[q, z] = out[q]
            return carry

        lax.fori_loop(low, high, body, 0)

    sections(f_ref, 0)
    pl.semaphore_wait(barrier, TILES - 1 + 6)
    scatter_start(0)

    def fill(d, carry):
        lanes = pl.ds(pl.multiple_of(d * chunk, chunk), chunk)
        for e in range(2):
            for k, ref in enumerate((area_ref, twist_ref, speed_ref, angle_ref)):
                bl_tx[d, e, k : k + 1, :] = ref[e : e + 1, lanes]
            for axis in range(3):
                bl_tx[d, e, 4 + axis : 5 + axis, :] = filt_ref[e, axis : axis + 1, lanes]
            bl_tx[d, e, 7:8, :] = jnp.zeros((1, chunk), F32)
        return carry

    lax.fori_loop(0, TILES, fill, 0)
    exchange_start(lambda to: bl_tx.at[to], bl_rx.at[me], bl_s, bl_r)

    lanes = pl.ds(pl.multiple_of(me * chunk, chunk), chunk)
    for s in range(SLOTS):
        codes = mc_ref[pl.ds(ids[s], 1), lanes]
        fraction_z = (codes % 8).astype(F32) / 8.0
        fraction_y = (codes // 8 % 8).astype(F32) / 8.0
        cell_z = codes // 64 % LEVELS
        cell_y = codes // (64 * LEVELS)
        weights_y = [peskin(corner - 1.0 - fraction_y) for corner in range(4)]
        weights_z = [peskin(corner - 1.0 - fraction_z) for corner in range(4)]
        gap = lax.broadcasted_iota(jnp.int32, (LEVELS, chunk), 0) - cell_z
        upward = jnp.zeros((LEVELS, chunk), F32)
        for corner in range(4):
            upward = jnp.where(gap == corner, weights_z[corner], upward)
        up_ref[s] = upward
        anchor = cell_y - firsts[s] * CY
        for part in range(8):
            gap = lax.broadcasted_iota(jnp.int32, (32, chunk), 0) + 32 * part - anchor
            across = jnp.zeros((32, chunk), F32)
            for corner in range(4):
                across = jnp.where(gap == corner, weights_y[corner], across)
            high, low = split(across)
            w_hi[s, 32 * part : 32 * part + 32, :] = high
            w_lo[s, 32 * part : 32 * part + 32, :] = low

    blade = {}
    x_ids = lax.broadcasted_iota(jnp.int32, (CX, CY), 0)
    y_ids = lax.broadcasted_iota(jnp.int32, (CX, CY), 1)
    last_filtered = None

    for step in range(steps):
        source = f_ref if step == 0 else fnext
        target = fo_ref if step == steps - 1 else fnext
        turn = 2 * step
        if step > 0:
            sections(source, turn)
            scatter_start(turn)
        collide_levels(source, 0, 8)
        scatter_finish(turn)
        collide_levels(source, 8, LEVELS)
        gather_wait(turn)

        sampled = [[], [], []]
        for s in range(SLOTS):
            wide = jnp.concatenate([window(turn, s, 0), window(turn, s, 1)], axis=1)
            high, low = split(wide)
            both = jnp.concatenate([high, low], axis=0)
            first_part = jnp.dot(both, w_hi[s], preferred_element_type=F32)
            second_part = jnp.dot(high, w_lo[s], preferred_element_type=F32)
            partial = first_part[:48] + first_part[48:] + second_part
            for axis in range(3):
                weighted = partial[axis * LEVELS : (axis + 1) * LEVELS] * up_ref[s]
                sampled[axis].append(jnp.sum(weighted, axis=0, keepdims=True))
        sampled = [jnp.concatenate(rows, axis=0) for rows in sampled]

        if step == 0:
            exchange_wait(bl_tx.at[0], bl_r, "recv")
            bl_rx[me] = bl_tx[me]
            picks = [bl_rx[owners[s], ranks[s]] for s in range(SLOTS)]
            rows = [
                jnp.concatenate([picks[s][k : k + 1] for s in range(SLOTS)], axis=0)
                for k in range(7)
            ]
            area, twist, speed, angle = rows[:4]
            filtered = rows[4:]
            sin_t = jnp.sin(angle)
            cos_t = jnp.cos(angle)
        filtered = [filtered[axis] + MIX * (sampled[axis] - filtered[axis]) for axis in range(3)]
        phase = jnp.concatenate(
            [jnp.full((1, chunk), pp_ref[ids[s], step], jnp.int32) for s in range(SLOTS)], axis=0
        )
        pitch = PITCH_AMP * jnp.sin(2.0 * math.pi * phase.astype(F32) / PHASES)
        axial = filtered[0]
        tangent = speed + sin_t * filtered[1] - cos_t * filtered[2]
        square = axial * axial + tangent * tangent
        magnitude = jnp.sqrt(square)
        sin_p = axial / magnitude
        cos_p = tangent / magnitude
        beta = twist + pitch
        sin_b = jnp.sin(beta)
        cos_b = jnp.cos(beta)
        sin_a = sin_p * cos_b - cos_p * sin_b
        cos_a = cos_p * cos_b + sin_p * sin_b
        lift = 2.0 * math.pi * sin_a * cos_a
        drag = 0.02 + sin_a * sin_a
        dynamic = 0.5 * area * square
        normal = dynamic * (lift * cos_p + drag * sin_p)
        tangential = dynamic * (lift * sin_p - drag * cos_p)
        loads = [normal, -tangential * sin_t, tangential * cos_t]

        turn = 2 * step + 1
        for s in range(SLOTS):
            live = jnp.full((1, chunk), valid[s], jnp.int32) > 0
            weighted = jnp.concatenate(
                [
                    up_ref[s] * jnp.where(live, -SPREAD * loads[axis][s : s + 1], 0.0)
                    for axis in range(3)
                ],
                axis=0,
            )
            high, low = split(weighted)
            both = jnp.concatenate([high, low], axis=0)
            contract = (((1,), (1,)), ((), ()))
            first_part = lax.dot_general(both, w_hi[s], contract, preferred_element_type=F32)
            second_part = lax.dot_general(high, w_lo[s], contract, preferred_element_type=F32)
            section = first_part[:48] + first_part[48:] + second_part
            for half in range(2):
                for block in range(6):
                    at = s * 96 + half * 48 + 8 * block
                    win_tx[turn, at // SHARD, at % SHARD : at % SHARD + 8, :] = section[
                        8 * block : 8 * block + 8, half * CY : half * CY + CY
                    ]
        scatter_start(turn)
        if step == steps - 1:
            for s in range(SLOTS):
                val_ref[s] = jnp.concatenate(
                    [value[s : s + 1] for value in loads + filtered + [phase.astype(F32)] * 2],
                    axis=0,
                )

            def answer(d, carry):
                for e in range(2):
                    total = jnp.zeros((8, chunk), F32)
                    for s in range(SLOTS):
                        mine = valid[s] * (owners[s] == d).astype(jnp.int32)
                        mine = mine * (ranks[s] == e).astype(jnp.int32)
                        total = jnp.where(
                            jnp.full((8, chunk), mine, jnp.int32) > 0, val_ref[s], total
                        )
                    ou_tx[d, e] = total
                return carry

            lax.fori_loop(0, TILES, answer, 0)
        scatter_finish(turn)
        if step == steps - 1:
            exchange_start(lambda to: ou_tx.at[to], ou_rx.at[me], ou_s, ou_r)
        gather_wait(turn)

        forces = []
        for s in range(SLOTS):
            first = jnp.broadcast_to(firsts[s], level_shape)
            halves = [window(turn, s, 0), window(turn, s, 1)]
            forces.append(
                [
                    jnp.where(first == me, halves[0][axis * LEVELS : (axis + 1) * LEVELS], 0.0)
                    + jnp.where(
                        first == me - 1, halves[1][axis * LEVELS : (axis + 1) * LEVELS], 0.0
                    )
                    for axis in range(3)
                ]
            )
        for s in range(SLOTS):
            force = []
            for axis in range(3):
                total = forces[s][axis]
                for other in range(SLOTS):
                    if other != s:
                        same = jnp.full(level_shape, planes[other] - planes[s], jnp.int32) == 0
                        total = total + jnp.where(same, forces[other][axis], 0.0)
                force.append(total)
            out = collide([plane_f[s, q] for q in range(NQ)], force)
            for q in range(NQ):
                plane_p[s, q] = out[q]

        masks = [x_ids == planes[s] for s in range(SLOTS)]

        def settle(z, carry):
            up, down = carry
            for q in range(NQ):
                slab = post[q, z]
                for s in range(SLOTS):
                    slab = jnp.where(masks[s], plane_p[s, q, pl.ds(z, 1), :], slab)
                post[q, z] = slab
                if q in Y_PLUS:
                    lane = Y_PLUS.index(q) * LEVELS + z
                    moved = pltpu.roll(slab, lax.rem(lane + 1, CY), axis=1)
                    up = jnp.where(y_ids == lane, moved, up)
                if q in Y_MINUS:
                    lane = Y_MINUS.index(q) * LEVELS + z
                    down = jnp.where(y_ids == lane, pltpu.roll(slab, lane, axis=1), down)
            return up, down

        nothing = jnp.zeros((CX, CY), F32)
        up, down = lax.fori_loop(0, LEVELS, settle, (nothing, nothing))
        ys_tx[step, 0] = up
        ys_tx[step, 1] = down
        for k, q in enumerate(X_PLUS):
            xs_tx[step, 0, k] = post[q, :, CX - 1, :]
        for k, q in enumerate(X_MINUS):
            xs_tx[step, 1, k] = post[q, :, 0, :]

        def send(src, dst, k, to):
            return pltpu.make_async_remote_copy(
                src_ref=src, dst_ref=dst, send_sem=ha_s.at[step, k], recv_sem=ha_r.at[step, k],
                device_id=to, device_id_type=MESH,
            )

        hops = [
            send(xs_tx.at[step, 0], xs_rx.at[step, 0], 0, {"gx": x_up}),
            send(xs_tx.at[step, 1], xs_rx.at[step, 1], 1, {"gx": x_dn}),
            send(ys_tx.at[step, 0, 8:16], cr_rx.at[step, 0], 4, {"gx": x_up, "gy": y_up}),
            send(ys_tx.at[step, 1, 0:8], cr_rx.at[step, 1], 5, {"gx": x_dn, "gy": y_dn}),
            send(ys_tx.at[step, 1, 8:16], cr_rx.at[step, 2], 6, {"gx": x_up, "gy": y_dn}),
            send(ys_tx.at[step, 0, 0:8], cr_rx.at[step, 3], 7, {"gx": x_dn, "gy": y_up}),
            send(ys_tx.at[step, 0], ys_rx.at[step, 0], 2, {"gy": y_up}),
            send(ys_tx.at[step, 1], ys_rx.at[step, 1], 3, {"gy": y_dn}),
        ]
        for hop in hops:
            hop.start()

        def stream(z, bottom, top):
            for q in range(NQ):
                cx, cy, cz = DIRS[q]
                if (cz == 1 and bottom) or (cz == -1 and top):
                    target[q, z] = post[OPPOSITE[q], z]
                    continue
                slab = post[q, z - cz]
                if cx:
                    slab = pltpu.roll(slab, cx % CX, axis=0)
                if cy:
                    slab = pltpu.roll(slab, cy % CY, axis=1)
                target[q, z] = slab

        stream(0, True, False)
        stream(LEVELS - 1, False, True)

        def stream_body(z, carry):
            stream(z, False, False)
            return carry

        lax.fori_loop(1, LEVELS - 1, stream_body, 0)
        for hop in hops:
            hop.wait_recv()

        packed = {}
        for q in Y_PLUS + Y_MINUS:
            cx, cy, cz = DIRS[q]
            column = ys_rx[step, 0 if cy == 1 else 1]
            if cx:
                corner = {(1, 1): 0, (-1, -1): 1, (1, -1): 2, (-1, 1): 3}[(cx, cy)]
                edge = cr_rx[step, corner, 7:8, :] if cx == 1 else cr_rx[step, corner, 0:1, :]
                column = pltpu.roll(column, cx % CX, axis=0)
                column = jnp.where(x_ids == (0 if cx == 1 else CX - 1), edge, column)
            packed[q] = column

        def edges(z, bottom, top):
            for q in range(NQ):
                cx, cy, cz = DIRS[q]
                if not (cx or cy) or (cz == -1 and bottom) or (cz == 1 and top):
                    continue
                if cx:
                    side, names = (0, X_PLUS) if cx == 1 else (1, X_MINUS)
                    row = xs_rx[step, side, names.index(q), pl.ds(z, 1), :]
                    at = 0 if cx == 1 else CX - 1
                if cx and not cy:
                    target[q, z + cz, at : at + 1, :] = row
                    continue
                slab = target[q, z + cz]
                if cx:
                    row = pltpu.roll(jnp.broadcast_to(row, (8, CY)), cy % CY, axis=1)[0:1]
                    slab = jnp.where(x_ids == at, row, slab)
                names = Y_PLUS if cy == 1 else Y_MINUS
                lane = names.index(q) * LEVELS + z
                to = 0 if cy == 1 else CY - 1
                moved = pltpu.roll(packed[q], lax.rem(to - lane + CY, CY), axis=1)
                target[q, z + cz] = jnp.where(y_ids == to, moved, slab)

        edges(0, True, False)
        edges(LEVELS - 1, False, True)

        def edges_body(z, carry):
            edges(z, False, False)
            return carry

        lax.fori_loop(1, LEVELS - 1, edges_body, 0)
        for hop in hops:
            hop.wait_send()

    exchange_wait(ou_tx.at[0], ou_r, "recv")
    ou_rx[me] = ou_tx[me]

    def place(d, carry):
        lanes = pl.ds(pl.multiple_of(d * chunk, chunk), chunk)
        for e in range(2):
            lo_ref[e, :, lanes] = ou_rx[d, e, 0:3, :]
            io_ref[e, :, lanes] = ou_rx[d, e, 3:6, :]
        return carry

    lax.fori_loop(0, TILES, place, 0)
    exchange_wait(bl_tx.at[0], bl_s, "send")
    exchange_wait(ou_tx.at[0], ou_s, "send")
    for turn in range(2 * steps):
        sends_done(turn)


def local(
    f_in, rotor_place, marker_cell, pitch_phase,
    blade_area, blade_twist, blade_speed, blade_angle, filt_in,
):
    steps = pitch_phase.shape[1]
    owned = filt_in.shape[2]
    markers = filt_in.shape[4]
    chunk = markers // TILES
    turns = 2 * steps
    field = f_in.shape
    vmem = pl.BlockSpec(memory_space=pltpu.VMEM)
    smem = pl.BlockSpec(memory_space=pltpu.SMEM)
    dma = pltpu.SemaphoreType.DMA
    scratch = [
        pltpu.VMEM(field, F32),
        pltpu.VMEM(field, F32),
        pltpu.VMEM((SLOTS, NQ, LEVELS, CY), F32),
        pltpu.VMEM((SLOTS, NQ, LEVELS, CY), F32),
        pltpu.VMEM((turns, REDUCERS, SHARD, CY), F32),
        pltpu.VMEM((turns, TILES, SHARD, CY), F32),
        pltpu.VMEM((turns, REDUCERS, SHARD, CY), F32),
        pltpu.VMEM((TILES, owned, 8, chunk), F32),
        pltpu.VMEM((TILES, owned, 8, chunk), F32),
        pltpu.VMEM((TILES, owned, 8, chunk), F32),
        pltpu.VMEM((TILES, owned, 8, chunk), F32),
        pltpu.VMEM((SLOTS, 2 * CY, chunk), jnp.bfloat16),
        pltpu.VMEM((SLOTS, 2 * CY, chunk), jnp.bfloat16),
        pltpu.VMEM((SLOTS, LEVELS, chunk), F32),
        pltpu.VMEM((SLOTS, 8, chunk), F32),
        pltpu.VMEM((steps, 2, 5, LEVELS, CY), F32),
        pltpu.VMEM((steps, 2, 5, LEVELS, CY), F32),
        pltpu.VMEM((steps, 2, CX, CY), F32),
        pltpu.VMEM((steps, 2, CX, CY), F32),
        pltpu.VMEM((steps, 4, 8, CY), F32),
        dma((turns, TILES)), dma((turns, TILES)), dma((turns, TILES)), dma((turns, TILES)),
        dma((TILES,)), dma((TILES,)), dma((TILES,)), dma((TILES,)),
        dma((steps, 8)), dma((steps, 8)),
    ]
    out = pl.pallas_call(
        mega,
        out_shape=(
            jax.ShapeDtypeStruct(field, F32),
            jax.ShapeDtypeStruct((owned, 3, markers), F32),
            jax.ShapeDtypeStruct((owned, 3, markers), F32),
        ),
        in_specs=[vmem, smem, vmem, smem, vmem, vmem, vmem, vmem, vmem],
        out_specs=(vmem, vmem, vmem),
        scratch_shapes=scratch,
        compiler_params=pltpu.CompilerParams(
            collective_id=0, has_side_effects=True, vmem_limit_bytes=56 * 1024 * 1024
        ),
        name="farm",
    )(
        f_in, rotor_place, marker_cell, pitch_phase,
        blade_area[0, 0], blade_twist[0, 0], blade_speed[0, 0], blade_angle[0, 0], filt_in[0, 0],
    )
    return out[0], out[1][None, None], out[2][None, None]


def solution(mesh):
    blade = P("gx", "gy", None, None)
    marker = P("gx", "gy", None, None, None)
    field = P(None, None, "gx", "gy")
    in_specs = (field, P(), P(), P(), blade, blade, blade, blade, marker)
    out_specs = (field, marker, marker)
    return jax.shard_map(local, mesh=mesh, in_specs=in_specs, out_specs=out_specs, check_vma=False)
```
